32 devices in a mesh: groups: 2 (over y), ctx: 4 (over x, core), head: 4 (over z).
Axes of the slice: x: 2, y: 2, z: 4, core: 2. Of those that a mesh axis runs over, the one named last changes fastest.
Arguments:
- queries: bfloat16 [1536, 8, 5, 128], P(('groups', 'ctx'), 'head'), parts along dimension 0, may hold values from -6 to 6
- keys_values: bfloat16 [1536, 8, 2, 128], P(('groups', 'ctx'), 'head'), parts along dimension 0, may hold values from -6 to 6
- prior_state: bfloat16 [16, 8256, 128], P(('groups', 'head'), 'ctx'), parts along dimension 0, may hold values from -224 to 224
- counts: int32 [2], P('groups'), parts along dimension 0, may hold values from 384 to 1535
- continuation: int32 [64], P('groups'), parts along dimension 0, may hold values from 0 to 75967
- query_table: bfloat16 [75968, 8, 5, 128], P('ctx', 'head'), may hold values from -6 to 6
- pair_table: bfloat16 [75968, 8, 2, 128], P('ctx', 'head'), may hold values from -6 to 6
Outputs:
- readout: bfloat16 [1536, 8, 5, 128], P(('groups', 'ctx'), 'head'), parts along dimension 0
- decode_out: bfloat16 [64, 8, 5, 128], P(('groups', 'ctx'), 'head'), parts along dimension 0
- decode_state: float32 [16, 8256, 128], P(('groups', 'head'), 'ctx'), parts along dimension 0
The draws below stay inside these ranges and needn't reach their ends.
There are 2 independent parts, one for each index of `groups`. The reference program is written for one: setup_inputs(seed, part) draws one part's arguments, and reference() takes and returns one part's arrays. A program takes and returns all parts, laid end to end along the dimension named above; an argument that names none is the same for every part. Nothing has to cross between parts.
All inputs are finite; a program needn't handle non-finite values.
Results may differ from the reference program's by a relative error of at most 0.0048.
The reference program's roundings to bfloat16 on the way count: a program that leaves them out, or rounds other values in their place, can miss the bound.
Values may be sent and summed in bfloat16 or wider, within the bound.
A program may use at most 256 MiB of HBM per device.

```python
import math
import jax
import jax.numpy as jnp
import numpy as np
from jax import lax

HD = 128
KV = 8
G = 5
DX = 8256
TOK_DEV = 192
TOKENS = 768
STEPS = 32
VOCAB = 75968


def with_ends(values, key, smallest, high):
    dims = values.shape
    spot = [jax.random.randint(jax.random.fold_in(key, axis), (), 0, dims[axis]) for axis in range(len(dims))]
    values = values.at[tuple(spot)].set(smallest)
    longest = dims.index(max(dims))
    spot[longest] = (spot[longest] + 1) % dims[longest]
    return values.at[tuple(spot)].set(high)


def block_scale(rng, shape, cuts, smallest, largest):
    level, own = 1.0, jax.random.fold_in(rng, 6)
    for axis_at, shards_of in cuts:
        draws = jnp.exp(jax.random.uniform(jax.random.fold_in(own, axis_at), (shards_of,), jnp.float32, smallest / len(cuts), largest / len(cuts)))
        level = level * jnp.repeat(draws, shape[axis_at] // shards_of).reshape([-1 if axis == axis_at else 1 for axis in range(len(shape))])
    return level


def ranked_wide(own_key, shape, count, skew):
    loads = [min(1 << octave, count + 1 - (1 << octave)) * (1 << 20) // math.isqrt((1 << octave) ** skew) + 1 for octave in range((count + 1).bit_length()) if 1 << octave <= count]
    spread = 1 + sum(loads) // (1 << 30)
    grid = np.cumsum(np.array([max(1, weight // spread) for weight in loads]))
    pick = jax.random.randint(jax.random.fold_in(own_key, 1), shape, 0, int(grid[len(loads) - 1]))
    start = jnp.left_shift(1, jnp.searchsorted(jnp.asarray(grid, jnp.int32), pick, side="right").astype(jnp.int32))
    rank = start - 1 + jax.random.randint(jax.random.fold_in(own_key, 4), shape, 0, 1 << 30) % jnp.minimum(start, count + 1 - start)
    return jax.random.permutation(jax.random.fold_in(own_key, 2), count)[rank].astype(jnp.int32)


def centred(key, shape, scale, bound, shards=(), held_as=jnp.bfloat16):
    result = jax.random.normal(key, shape, jnp.float32) * scale
    if len(shards) > 0:
        result = block_scale(key, shape, shards, -0.22, 0.18) * result
    return jnp.clip(result, min=-bound, max=bound).astype(held_as)


def setup_inputs(seed: int = 0, part: int = 0) -> dict:
    keys = jax.random.split(jax.random.key(seed), 8)
    part_splits = jax.random.split(jax.random.fold_in(keys[7], part), 8)
    queries = centred(part_splits[0], (TOKENS, KV, G, HD), 1.0, 6.0, ((0, 4), (1, 4)))
    keys_values = centred(part_splits[1], (TOKENS, KV, 2, HD), 1.0, 6.0, ((0, 4), (1, 4)))
    prior_state = centred(part_splits[2], (KV, DX, HD), ((2 * TOKENS) ** 0.5), 224.0, ((0, 4), (1, 4)))
    counts = jax.random.randint(part_splits[3], (1,), TOKENS // 2, 2 * TOKENS).astype(jnp.int32)
    continuation = with_ends(ranked_wide(part_splits[4], (STEPS,), VOCAB, 2), jax.random.fold_in(part_splits[4], 3), 0, VOCAB - 1).astype(jnp.int32)
    query_table = centred(keys[5], (VOCAB, KV, G, HD), 1.0, 6.0, ((0, 4), (1, 4)))
    pair_table = centred(keys[6], (VOCAB, KV, 2, HD), 1.0, 6.0, ((0, 4), (1, 4)))
    return {"queries": queries, "keys_values": keys_values, "prior_state": prior_state, "counts": counts, "continuation": continuation, "query_table": query_table, "pair_table": pair_table}


ROOT_TWO = 2.0 ** 0.5
NUM_BLOCKS = 8

def expand_range(values, first_offset, how_many):
    width = values.shape[-1]
    doubled = jnp.concatenate([values, values], axis=-1)
    scaled = doubled * ROOT_TWO
    pieces = []
    for offset in range(first_offset, first_offset + how_many):
        partner = doubled if offset == 0 else scaled
        pieces.append(values * partner[..., offset:offset + width])
    return jnp.concatenate(pieces, axis=-1)

def expand_tail(values):
    half_width = values.shape[-1] // 2
    return values[..., :half_width] * (values[..., half_width:] * ROOT_TWO)

def feature_piece(values, number):
    head_size = values.shape[-1]
    if number == NUM_BLOCKS:
        return expand_tail(values)
    per_block = head_size // 2 // NUM_BLOCKS
    return expand_range(values, number * per_block, per_block)

def expand_all(values):
    return jnp.concatenate([feature_piece(values, number) for number in range(NUM_BLOCKS + 1)], axis=-1)

def causal_sum(query_rows, key_rows, value_rows):
    scores = jnp.einsum('tgd,sd->gts', query_rows.astype(jnp.float32), key_rows.astype(jnp.float32))
    allowed = jnp.arange(query_rows.shape[0], dtype=jnp.int32)[:, None] >= jnp.arange(key_rows.shape[0], dtype=jnp.int32)[None, :]
    weights = jnp.where(allowed[None], scores * scores / HD, 0.0).astype(jnp.bfloat16)
    return jnp.einsum('gts,sd->tgd', weights.astype(jnp.float32), value_rows.astype(jnp.float32))

def head_window(packed, start_count):
    head_queries, head_pairs, head_prior, step_queries, step_pairs = packed
    block_queries_all = head_queries.reshape(-1, TOK_DEV, G, HD)
    block_pairs_all = head_pairs.reshape(-1, TOK_DEV, 2, HD)
    block_count = block_queries_all.shape[0]

    def advance(running, block):
        block_queries, block_pairs, block_number = block
        phi_keys = expand_all(block_pairs[:, 0].astype(jnp.float32)).astype(jnp.bfloat16)
        phi_queries = expand_all(block_queries.astype(jnp.float32)).astype(jnp.bfloat16)
        carried = jnp.dot(phi_queries.reshape(-1, DX), running.astype(jnp.bfloat16), preferred_element_type=jnp.float32).reshape(TOK_DEV, G, HD)
        own_sum = causal_sum(block_queries, block_pairs[:, 0], block_pairs[:, 1])
        positions = start_count + block_number * TOK_DEV + jnp.arange(TOK_DEV, dtype=jnp.int32) + 1
        output = ((carried / HD + own_sum) / jnp.sqrt(positions.astype(jnp.float32))[:, None, None]).astype(jnp.bfloat16)
        running = running + jnp.dot(phi_keys.T, block_pairs[:, 1], preferred_element_type=jnp.float32)
        return (running, output)
    final_state, outputs = lax.scan(advance, head_prior.astype(jnp.float32), (block_queries_all, block_pairs_all, jnp.arange(block_count, dtype=jnp.int32)))
    readout = outputs.reshape(TOKENS, G, HD)
    step_phi_queries = expand_all(step_queries.astype(jnp.float32)).astype(jnp.bfloat16)
    step_carried = jnp.dot(step_phi_queries.reshape(-1, DX), final_state.astype(jnp.bfloat16), preferred_element_type=jnp.float32).reshape(STEPS, G, HD)
    step_own = causal_sum(step_queries, step_pairs[:, 0], step_pairs[:, 1])
    step_positions = start_count + TOKENS + jnp.arange(STEPS, dtype=jnp.int32) + 1
    decode_out = ((step_carried / HD + step_own) / jnp.sqrt(step_positions.astype(jnp.float32))[:, None, None]).astype(jnp.bfloat16)
    step_phi_keys = expand_all(step_pairs[:, 0].astype(jnp.float32)).astype(jnp.bfloat16)
    decode_state = final_state + jnp.dot(step_phi_keys.T, step_pairs[:, 1], preferred_element_type=jnp.float32)
    return (readout, decode_out, decode_state)

def reference(queries, keys_values, prior_state, counts, continuation, query_table, pair_table):
    step_queries = jnp.take(query_table, continuation, axis=0)
    step_pairs = jnp.take(pair_table, continuation, axis=0)
    start_count = counts[0]

    def per_head(packed):
        return head_window(packed, start_count)
    readout, decode_out, decode_state = lax.map(per_head, (jnp.swapaxes(queries, 0, 1), jnp.swapaxes(keys_values, 0, 1), prior_state, jnp.swapaxes(step_queries, 0, 1), jnp.swapaxes(step_pairs, 0, 1)))
    return (jnp.swapaxes(readout, 0, 1), jnp.swapaxes(decode_out, 0, 1), decode_state)
```

```python
import functools

import jax
import jax.numpy as jnp
from jax import lax
from jax.experimental import pallas as pl
from jax.experimental.pallas import tpu as pltpu
from jax.sharding import PartitionSpec as P

ROOT_TWO = 2.0**0.5
MESH = pl.DeviceIdType.MESH
TILE = 256
LANES = 128


def round_up(number, multiple):
    return (number + multiple - 1) // multiple * multiple


def pick_kernel(ids_ref, query_table, pair_table, query_out, pair_out, query_sem, pair_sem):
    step_count = query_out.shape[0]

    def copies(step):
        row = ids_ref[step]
        return (
            pltpu.make_async_copy(query_table.at[row], query_out.at[step], query_sem.at[step]),
            pltpu.make_async_copy(pair_table.at[row], pair_out.at[step], pair_sem.at[step]),
        )

    for step in range(step_count):
        for copy in copies(step):
            copy.start()
    for step in range(step_count):
        for copy in copies(step):
            copy.wait()


def pick_rows(ids, query_table, pair_table):
    steps = ids.shape[0]
    return pl.pallas_call(
        pick_kernel,
        out_shape=(
            jax.ShapeDtypeStruct((steps,) + query_table.shape[1:], query_table.dtype),
            jax.ShapeDtypeStruct((steps,) + pair_table.shape[1:], pair_table.dtype),
        ),
        in_specs=[
            pl.BlockSpec(memory_space=pltpu.SMEM),
            pl.BlockSpec(memory_space=pl.ANY),
            pl.BlockSpec(memory_space=pl.ANY),
        ],
        out_specs=(
            pl.BlockSpec(memory_space=pltpu.VMEM),
            pl.BlockSpec(memory_space=pltpu.VMEM),
        ),
        scratch_shapes=[pltpu.SemaphoreType.DMA((steps,)), pltpu.SemaphoreType.DMA((steps,))],
        name="pick_rows",
    )(ids, query_table, pair_table)


def main_kernel(
    sizes,
    queries,
    blob,
    prior,
    out,
    state,
    land_blob,
    land_prior,
    query_rows,
    step_rows,
    key_rows,
    value_rows,
    turned,
    blob_send,
    blob_recv,
    prior_send,
    prior_recv,
    local_sem,
):
    n, heads, group, tok_rows, step_count, rows_valid = sizes
    chips = n // 2
    per_shard = step_count // n
    window_rows = tok_rows * group
    window = n * tok_rows
    prior_rows = prior.shape[1]
    blocks = land_prior.shape[2] // LANES
    row_tiles = out.shape[1] // TILE
    padded_keys = key_rows.shape[1]
    me = lax.axis_index("ctx")
    core = lax.rem(me, 2)
    partner = me + 1 - 2 * core

    def across(step):
        return lax.rem(me + 2 * step, n)

    def twin(index):
        return index + 1 - 2 * lax.rem(index, 2)

    barrier = pltpu.get_barrier_semaphore()
    pl.semaphore_signal(barrier, inc=1, device_id={"ctx": partner}, device_id_type=MESH)
    for step in range(1, chips):
        pl.semaphore_signal(barrier, inc=1, device_id={"ctx": across(step)}, device_id_type=MESH)
    pl.semaphore_wait(barrier, chips)

    def blob_copy(src, source, slot, target):
        return pltpu.make_async_remote_copy(
            src_ref=src,
            dst_ref=land_blob.at[source],
            send_sem=blob_send.at[slot],
            recv_sem=blob_recv.at[source],
            device_id={"ctx": target},
            device_id_type=MESH,
        )

    def prior_copy(src, source, head, slot, target):
        return pltpu.make_async_remote_copy(
            src_ref=src,
            dst_ref=land_prior.at[source, head, pl.ds(0, prior_rows)],
            send_sem=prior_send.at[slot, head],
            recv_sem=prior_recv.at[source, head],
            device_id={"ctx": target},
            device_id_type=MESH,
        )

    def blob_own(slot):
        return blob_copy(blob, me, slot, partner if slot == 0 else across(slot))

    def blob_forward(step):
        source = across(step)
        return blob_copy(land_blob.at[source], source, chips - 1 + step, partner)

    def prior_own(slot, head):
        target = partner if slot == 0 else across(slot)
        return prior_copy(prior.at[head], me, head, slot, target)

    def prior_forward(step, head):
        source = across(step)
        return prior_copy(
            land_prior.at[source, head, pl.ds(0, prior_rows)],
            source,
            head,
            chips - 1 + step,
            partner,
        )

    for slot in list(range(1, chips)) + [0]:
        blob_own(slot).start()
    for head in range(heads):
        for slot in list(range(1, chips)) + [0]:
            prior_own(slot, head).start()
    own_blob = pltpu.make_async_copy(blob, land_blob.at[me], local_sem.at[0])
    own_prior = pltpu.make_async_copy(
        prior, land_prior.at[me, :, pl.ds(0, prior_rows)], local_sem.at[1]
    )
    own_blob.start()
    own_prior.start()

    if prior_rows < blocks * LANES:
        rest = blocks * LANES - prior_rows
        for source in range(n):
            for head in range(heads):
                land_prior[source, head, pl.ds(prior_rows, rest), :] = jnp.zeros(
                    (rest, LANES), jnp.bfloat16
                )
    out[...] = jnp.zeros_like(out)
    for head in range(heads):
        query_rows[head, pl.ds(0, window_rows), :] = queries[head].astype(jnp.float32)
        query_rows[head, pl.ds(window_rows, out.shape[1] - window_rows), :] = jnp.zeros(
            (out.shape[1] - window_rows, LANES), jnp.float32
        )
        spare = padded_keys - window - step_count
        if spare > 0:
            key_rows[head, pl.ds(window + step_count, spare), :] = jnp.zeros(
                (spare, LANES), jnp.bfloat16
            )
            value_rows[head, pl.ds(window + step_count, spare), :] = jnp.zeros(
                (spare, LANES), jnp.bfloat16
            )

    def place(source):
        first = source * rows_valid
        return lax.div(first, LANES), lax.rem(first, LANES)

    def carry_tile(source, head, tile):
        first_offset, lead = place(source)
        rows = pl.ds(pl.multiple_of(tile * TILE, TILE), TILE)
        values = query_rows[head, rows, :]
        scaled = values * ROOT_TWO
        lane = lax.broadcasted_iota(jnp.int32, (TILE, LANES), 1)
        early = lane < LANES - lead

        def turn(array, amount):
            shift = lax.rem(2 * LANES - lax.rem(amount, LANES), LANES)
            return pltpu.roll(array, shift, 1)

        here = turn(values, lead)
        near = turn(scaled, lead + first_offset)
        pieces = []
        for block in range(blocks):
            far = turn(scaled, lead + first_offset + block + 1)
            partner_values = jnp.where(early, near, far)
            if block == 0:
                plain = jnp.logical_and(early, first_offset == 0)
                partner_values = jnp.where(plain, here, partner_values)
            pieces.append((here * partner_values).astype(jnp.bfloat16))
            near = far
        features = jnp.concatenate(pieces, axis=1)
        out[head, rows, :] += jnp.dot(
            features, land_prior[source, head], preferred_element_type=jnp.float32
        )

    def carry(source, head, first_tile, last_tile):
        @pl.loop(first_tile, last_tile)
        def _(tile):
            carry_tile(source, head, tile)

    full_tiles = window_rows // TILE
    own_prior.wait()
    for head in range(heads):
        carry(me, head, 0, full_tiles)

    own_blob.wait()
    blob_copy(blob, partner, 0, partner).wait_recv()
    for step in range(1, chips):
        blob_copy(blob, across(step), 0, partner).wait_recv()
        blob_forward(step).start()
    for step in range(1, chips):
        blob_copy(blob, twin(across(step)), 0, partner).wait_recv()

    for head in range(heads):
        for source in range(n):
            key_rows[head, pl.ds(source * tok_rows, tok_rows), :] = land_blob[
                source, head, pl.ds(0, tok_rows), :
            ]
            value_rows[head, pl.ds(source * tok_rows, tok_rows), :] = land_blob[
                source, heads + head, pl.ds(0, tok_rows), :
            ]

        def picked(plane, first, count):
            total = land_blob[0, plane, pl.ds(first, count), :].astype(jnp.float32)
            for source in range(1, n):
                total += land_blob[source, plane, pl.ds(first, count), :].astype(jnp.float32)
            return total

        key_rows[head, pl.ds(window, step_count), :] = picked(head, tok_rows, step_count).astype(
            jnp.bfloat16
        )
        value_rows[head, pl.ds(window, step_count), :] = picked(
            heads + head, tok_rows, step_count
        ).astype(jnp.bfloat16)
        half = step_count * group // 2
        for side in range(2):
            step_rows[head, pl.ds(side * half, half), :] = picked(
                2 * head + side, tok_rows + step_count, half
            )
        own_steps = per_shard * group
        query_rows[head, pl.ds(window_rows, own_steps), :] = step_rows[
            head, pl.ds(me * own_steps, own_steps), :
        ]

    for head in range(heads):
        carry(me, head, full_tiles, row_tiles)
        prior_copy(prior.at[head], partner, head, 0, partner).wait_recv()
        carry(partner, head, 0, row_tiles)

    first_offset, lead = place(me)
    identity = (
        lax.broadcasted_iota(jnp.int32, (LANES, LANES), 0)
        == lax.broadcasted_iota(jnp.int32, (LANES, LANES), 1)
    ).astype(jnp.bfloat16)
    contract_last = (((1,), (1,)), ((), ()))
    for head in range(heads):
        keys_turned = lax.dot_general(
            identity, key_rows[head], contract_last, preferred_element_type=jnp.float32
        )
        chunks = padded_keys // LANES
        for chunk in range(chunks):
            piece = keys_turned[:, chunk * LANES : (chunk + 1) * LANES]
            turned[head, chunk, pl.ds(0, LANES), :] = piece
            turned[head, chunk, pl.ds(LANES, LANES), :] = piece

        def state_block(block):
            row = lax.broadcasted_iota(jnp.int32, (LANES, LANES), 0)
            early = row < LANES - lead
            plain = jnp.logical_and(early, first_offset + block == 0)
            factor = jnp.where(plain, 1.0, ROOT_TWO)
            near_row = lax.rem(lead + first_offset + block, LANES)
            far_row = lax.rem(lead + first_offset + block + 1, LANES)
            pieces = []
            for chunk in range(chunks):
                here = turned[head, chunk, pl.ds(lead, LANES), :]
                near = turned[head, chunk, pl.ds(near_row, LANES), :]
                far = turned[head, chunk, pl.ds(far_row, LANES), :]
                both = jnp.where(early, near, far) * factor
                pieces.append((here * both).astype(jnp.bfloat16))
            features = jnp.concatenate(pieces, axis=1)
            return jnp.dot(features, value_rows[head], preferred_element_type=jnp.float32)

        whole_blocks = prior_rows // LANES

        @pl.loop(0, whole_blocks)
        def _(block):
            state[head, pl.ds(pl.multiple_of(block * LANES, LANES), LANES), :] = state_block(block)

        rest = prior_rows - whole_blocks * LANES
        if rest > 0:
            state[head, pl.ds(whole_blocks * LANES, rest), :] = state_block(whole_blocks)[:rest]

        @pl.loop(0, row_tiles)
        def _(tile):
            rows = pl.ds(pl.multiple_of(tile * TILE, TILE), TILE)
            scores = lax.dot_general(
                query_rows[head, rows, :].astype(jnp.bfloat16),
                key_rows[head],
                contract_last,
                preferred_element_type=jnp.float32,
            )
            local = tile * TILE + lax.broadcasted_iota(jnp.int32, (TILE, 1), 0)
            position = jnp.where(
                local < window_rows,
                local + me * window_rows,
                local - window_rows + window * group + me * (per_shard * group),
            )
            key_index = lax.broadcasted_iota(jnp.int32, scores.shape, 1)
            allowed = position >= key_index * group
            weights = jnp.where(allowed, scores * scores, 0.0).astype(jnp.bfloat16)
            out[head, rows, :] += jnp.dot(
                weights, value_rows[head], preferred_element_type=jnp.float32
            )

    for step in range(1, chips):
        source = across(step)
        for head in range(heads):
            prior_copy(prior.at[head], source, head, 0, partner).wait_recv()
            prior_forward(step, head).start()
            carry(source, head, 0, row_tiles)
            prior_copy(prior.at[head], twin(source), head, 0, partner).wait_recv()
            carry(twin(source), head, 0, row_tiles)

    for slot in range(chips):
        blob_own(slot).wait_send()
        for head in range(heads):
            prior_own(slot, head).wait_send()
    for step in range(1, chips):
        blob_forward(step).wait_send()
        for head in range(heads):
            prior_forward(step, head).wait_send()


def combine(sizes, queries, blob, prior, out_rows):
    n, heads, group, tok_rows, step_count, rows_valid = sizes
    prior_rows = prior.shape[1]
    padded_rows = round_up(prior_rows, LANES)
    padded_keys = round_up(n * tok_rows + step_count, LANES)
    slots = 2 * (n // 2) - 1
    vmem = pl.BlockSpec(memory_space=pltpu.VMEM)
    return pl.pallas_call(
        functools.partial(main_kernel, sizes),
        out_shape=(
            jax.ShapeDtypeStruct((heads, out_rows, LANES), jnp.float32),
            jax.ShapeDtypeStruct((heads, prior_rows, LANES), jnp.float32),
        ),
        in_specs=[vmem] * 3,
        out_specs=(vmem, vmem),
        scratch_shapes=[
            pltpu.VMEM((n,) + blob.shape, jnp.bfloat16),
            pltpu.VMEM((n, heads, padded_rows, LANES), jnp.bfloat16),
            pltpu.VMEM((heads, out_rows, LANES), jnp.float32),
            pltpu.VMEM((heads, step_count * group, LANES), jnp.float32),
            pltpu.VMEM((heads, padded_keys, LANES), jnp.bfloat16),
            pltpu.VMEM((heads, padded_keys, LANES), jnp.bfloat16),
            pltpu.VMEM((heads, padded_keys // LANES, 2 * LANES, LANES), jnp.float32),
            pltpu.SemaphoreType.DMA((slots,)),
            pltpu.SemaphoreType.DMA((n,)),
            pltpu.SemaphoreType.DMA((slots, heads)),
            pltpu.SemaphoreType.DMA((n, heads)),
            pltpu.SemaphoreType.DMA((2,)),
        ],
        compiler_params=pltpu.CompilerParams(
            collective_id=0, has_side_effects=True, vmem_limit_bytes=56 * 2**20
        ),
        name="combine",
    )(queries, blob, prior)


def on_device(queries, keys_values, prior_state, counts, continuation, query_table, pair_table):
    tok_rows, heads, group, head_size = queries.shape
    n = lax.axis_size("ctx")
    shard_index = lax.axis_index("ctx")
    step_count = continuation.shape[0]
    per_shard = step_count // n
    rows_valid = prior_state.shape[1]

    vocab_rows = query_table.shape[0]
    local_ids = continuation - shard_index * vocab_rows
    inside = (local_ids >= 0) & (local_ids < vocab_rows)
    safe_ids = jnp.clip(local_ids, 0, vocab_rows - 1)
    query_pick, pair_pick = pick_rows(safe_ids, query_table.transpose(0, 2, 1, 3), pair_table)
    mask = inside[:, None, None, None]
    query_pick = jnp.where(mask, query_pick, jnp.zeros_like(query_pick))
    pair_pick = jnp.where(mask, pair_pick, jnp.zeros_like(pair_pick))

    window_planes = keys_values.transpose(2, 1, 0, 3).reshape(2 * heads, tok_rows, head_size)
    step_planes = pair_pick.transpose(2, 1, 0, 3)
    step_planes = step_planes.reshape(2 * heads, step_count, head_size)
    query_planes = query_pick.transpose(2, 0, 1, 3).reshape(
        2 * heads, step_count * group // 2, head_size
    )
    blob = jnp.concatenate([window_planes, step_planes, query_planes], axis=1)
    query_planes = queries.transpose(1, 0, 2, 3).reshape(heads, tok_rows * group, head_size)
    prior_rows = round_up(rows_valid, 16)
    prior = prior_state
    if prior_rows > rows_valid:
        prior = jnp.pad(prior_state, ((0, 0), (0, prior_rows - rows_valid), (0, 0)))
    out_rows = round_up((tok_rows + per_shard) * group, TILE)
    sizes = (n, heads, group, tok_rows, step_count, rows_valid)
    total, added = combine(sizes, query_planes, blob, prior, out_rows)

    decode_state = prior_state.astype(jnp.float32) + added[:, :rows_valid]

    def finish(rows, first_position):
        count = rows.shape[1] // group
        positions = first_position + jnp.arange(count, dtype=jnp.int32) + 1
        scale = 1.0 / (head_size * jnp.sqrt(positions.astype(jnp.float32)))
        rows = rows.reshape(heads, count, group, head_size) * scale[None, :, None, None]
        return rows.astype(jnp.bfloat16).transpose(1, 0, 2, 3)

    window_rows = tok_rows * group
    readout = finish(total[:, :window_rows], counts[0] + shard_index * tok_rows)
    decode_out = finish(
        total[:, window_rows : window_rows + per_shard * group],
        counts[0] + n * tok_rows + shard_index * per_shard,
    )
    return (readout, decode_out, decode_state)


def solution(mesh):
    in_specs = (
        P(("groups", "ctx"), "head", None, None),
        P(("groups", "ctx"), "head", None, None),
        P(("groups", "head"), "ctx", None),
        P("groups"),
        P("groups"),
        P("ctx", "head", None, None),
        P("ctx", "head", None, None),
    )
    out_specs = (
        P(("groups", "ctx"), "head", None, None),
        P(("groups", "ctx"), "head", None, None),
        P(("groups", "head"), "ctx", None),
    )
    return jax.shard_map(
        on_device, mesh=mesh, in_specs=in_specs, out_specs=out_specs, check_vma=False
    )
```

```python
import functools

import jax
import jax.numpy as jnp
from jax import lax
from jax.experimental import pallas as pl
from jax.experimental.pallas import tpu as pltpu
from jax.sharding import PartitionSpec as P

ROOT_TWO = 2.0**0.5
MESH = pl.DeviceIdType.MESH
TILE = 256
LANES = 128


def round_up(number, multiple):
    return (number + multiple - 1) // multiple * multiple


def pick_kernel(ids_ref, query_table, pair_table, query_out, pair_out, query_sem, pair_sem):
    step_count = query_out.shape[0]

    def copies(step):
        row = ids_ref[step]
        return (
            pltpu.make_async_copy(query_table.at[row], query_out.at[step], query_sem.at[step]),
            pltpu.make_async_copy(pair_table.at[row], pair_out.at[step], pair_sem.at[step]),
        )

    for step in range(step_count):
        for copy in copies(step):
            copy.start()
    for step in range(step_count):
        for copy in copies(step):
            copy.wait()


def pick_rows(ids, query_table, pair_table):
    steps = ids.shape[0]
    return pl.pallas_call(
        pick_kernel,
        out_shape=(
            jax.ShapeDtypeStruct((steps,) + query_table.shape[1:], query_table.dtype),
            jax.ShapeDtypeStruct((steps,) + pair_table.shape[1:], pair_table.dtype),
        ),
        in_specs=[
            pl.BlockSpec(memory_space=pltpu.SMEM),
            pl.BlockSpec(memory_space=pl.ANY),
            pl.BlockSpec(memory_space=pl.ANY),
        ],
        out_specs=(
            pl.BlockSpec(memory_space=pltpu.VMEM),
            pl.BlockSpec(memory_space=pltpu.VMEM),
        ),
        scratch_shapes=[pltpu.SemaphoreType.DMA((steps,)), pltpu.SemaphoreType.DMA((steps,))],
        name="pick_rows",
    )(ids, query_table, pair_table)


def main_kernel(
    sizes,
    queries,
    blob,
    prior,
    out,
    state,
    land_blob,
    land_prior,
    query_rows,
    query_plain,
    query_scaled,
    prior_turned,
    total_turned,
    step_rows,
    key_rows,
    value_rows,
    turned,
    blob_send,
    blob_recv,
    prior_send,
    prior_recv,
    local_sem,
):
    n, heads, group, tok_rows, step_count, rows_valid = sizes
    chips = n // 2
    per_shard = step_count // n
    window_rows = tok_rows * group
    window = n * tok_rows
    prior_rows = prior.shape[1]
    shifted = prior_rows == rows_valid
    state_rows = state.shape[1]
    blocks = land_prior.shape[2] // LANES
    row_tiles = out.shape[1] // TILE
    padded_keys = key_rows.shape[1]
    me = lax.axis_index("ctx")
    core = lax.rem(me, 2)
    partner = me + 1 - 2 * core

    def across(step):
        return lax.rem(me + 2 * step, n)

    def twin(index):
        return index + 1 - 2 * lax.rem(index, 2)

    barrier = pltpu.get_barrier_semaphore()
    pl.semaphore_signal(barrier, inc=1, device_id={"ctx": partner}, device_id_type=MESH)
    for step in range(1, chips):
        pl.semaphore_signal(barrier, inc=1, device_id={"ctx": across(step)}, device_id_type=MESH)
    pl.semaphore_wait(barrier, chips)

    def blob_copy(src, source, slot, target):
        return pltpu.make_async_remote_copy(
            src_ref=src,
            dst_ref=land_blob.at[source],
            send_sem=blob_send.at[slot],
            recv_sem=blob_recv.at[source],
            device_id={"ctx": target},
            device_id_type=MESH,
        )

    def landing(source):
        first = pl.multiple_of(lax.rem(source * rows_valid, LANES), 16) if shifted else 0
        return pl.ds(first, prior_rows)

    def prior_copy(src, source, head, slot, target):
        return pltpu.make_async_remote_copy(
            src_ref=src,
            dst_ref=land_prior.at[source, head, landing(source)],
            send_sem=prior_send.at[slot, head],
            recv_sem=prior_recv.at[source, head],
            device_id={"ctx": target},
            device_id_type=MESH,
        )

    def blob_own(slot):
        return blob_copy(blob, me, slot, partner if slot == 0 else across(slot))

    def blob_forward(step):
        source = across(step)
        return blob_copy(land_blob.at[source], source, chips - 1 + step, partner)

    def prior_own(slot, head):
        target = partner if slot == 0 else across(slot)
        return prior_copy(prior.at[head], me, head, slot, target)

    def prior_forward(step, head):
        source = across(step)
        return prior_copy(
            land_prior.at[source, head, landing(source)],
            source,
            head,
            chips - 1 + step,
            partner,
        )

    for slot in list(range(1, chips)) + [0]:
        blob_own(slot).start()
    for head in range(heads):
        for slot in list(range(1, chips)) + [0]:
            prior_own(slot, head).start()
    own_blob = pltpu.make_async_copy(blob, land_blob.at[me], local_sem.at[0])
    own_prior = pltpu.make_async_copy(
        prior, land_prior.at[me, :, landing(me)], local_sem.at[1]
    )
    own_blob.start()
    own_prior.start()

    if shifted:
        for source in range(n):
            lead_rows = source * rows_valid % LANES
            for first, last in (
                (0, lead_rows),
                (lead_rows + prior_rows, blocks * LANES),
            ):
                if last > first:
                    for head in range(heads):
                        land_prior[source, head, pl.ds(first, last - first), :] = jnp.zeros(
                            (last - first, LANES), jnp.bfloat16
                        )
    total_turned[...] = jnp.zeros_like(total_turned)
    for head in range(heads):
        query_rows[head, pl.ds(0, window_rows), :] = queries[head]
        query_rows[head, pl.ds(window_rows, out.shape[1] - window_rows), :] = jnp.zeros(
            (out.shape[1] - window_rows, LANES), jnp.bfloat16
        )
        spare = padded_keys - window - step_count
        if spare > 0:
            key_rows[head, pl.ds(window + step_count, spare), :] = jnp.zeros(
                (spare, LANES), jnp.bfloat16
            )
            value_rows[head, pl.ds(window + step_count, spare), :] = jnp.zeros(
                (spare, LANES), jnp.bfloat16
            )

    def place(source):
        first = source * rows_valid
        return lax.div(first, LANES), lax.rem(first, LANES)

    identity = (
        lax.broadcasted_iota(jnp.int32, (LANES, LANES), 0)
        == lax.broadcasted_iota(jnp.int32, (LANES, LANES), 1)
    ).astype(jnp.bfloat16)
    contract_last = (((1,), (1,)), ((), ()))

    def transposed(rows):
        return lax.dot_general(identity, rows, contract_last, preferred_element_type=jnp.float32)

    chunks_per_tile = TILE // LANES

    def turn_queries(head, first_tile, last_tile):
        for chunk in range(first_tile * chunks_per_tile, last_tile * chunks_per_tile):
            piece = transposed(query_rows[head, pl.ds(chunk * LANES, LANES), :])
            scaled = piece * ROOT_TWO
            query_plain[head, chunk] = piece
            query_scaled[head, chunk, pl.ds(0, LANES), :] = scaled
            query_scaled[head, chunk, pl.ds(LANES, LANES), :] = scaled

    def carry_tile(source, head, tile):
        first_offset, _ = place(source)
        columns = []
        for side in range(chunks_per_tile):
            chunk = tile * chunks_per_tile + side
            here = query_plain[head, chunk]
            pieces = []
            for block in range(blocks):
                row = lax.rem(first_offset + block, LANES)
                other = query_scaled[head, chunk, pl.ds(row, LANES), :]
                if block == 0:
                    other = jnp.where(first_offset == 0, here, other)
                pieces.append((here * other).astype(jnp.bfloat16))
            columns.append(jnp.concatenate(pieces, axis=0))
        features = jnp.concatenate(columns, axis=1)
        total_turned[head, tile] += jnp.dot(
            prior_turned[...], features, preferred_element_type=jnp.float32
        )

    def carry(source, head, first_tile, last_tile):
        prior_turned[...] = transposed(land_prior[source, head]).astype(jnp.bfloat16)

        @pl.loop(first_tile, last_tile)
        def _(tile):
            carry_tile(source, head, tile)

    full_tiles = window_rows // TILE
    own_prior.wait()
    for head in range(heads):
        turn_queries(head, 0, full_tiles)
        carry(me, head, 0, full_tiles)

    own_blob.wait()
    blob_copy(blob, partner, 0, partner).wait_recv()
    for step in range(1, chips):
        blob_copy(blob, across(step), 0, partner).wait_recv()
        blob_forward(step).start()
    for step in range(1, chips):
        blob_copy(blob, twin(across(step)), 0, partner).wait_recv()

    for head in range(heads):
        for source in range(n):
            key_rows[head, pl.ds(source * tok_rows, tok_rows), :] = land_blob[
                source, head, pl.ds(0, tok_rows), :
            ]
            value_rows[head, pl.ds(source * tok_rows, tok_rows), :] = land_blob[
                source, heads + head, pl.ds(0, tok_rows), :
            ]

        def picked(plane, first, count):
            total = land_blob[0, plane, pl.ds(first, count), :].astype(jnp.float32)
            for source in range(1, n):
                total += land_blob[source, plane, pl.ds(first, count), :].astype(jnp.float32)
            return total

        key_rows[head, pl.ds(window, step_count), :] = picked(head, tok_rows, step_count).astype(
            jnp.bfloat16
        )
        value_rows[head, pl.ds(window, step_count), :] = picked(
            heads + head, tok_rows, step_count
        ).astype(jnp.bfloat16)
        half = step_count * group // 2
        for side in range(2):
            step_rows[head, pl.ds(side * half, half), :] = picked(
                2 * head + side, tok_rows + step_count, half
            )
        own_steps = per_shard * group
        own_rows = step_rows[head, pl.ds(me * own_steps, own_steps), :]
        query_rows[head, pl.ds(window_rows, own_steps), :] = own_rows.astype(jnp.bfloat16)
        turn_queries(head, full_tiles, row_tiles)

    for head in range(heads):
        carry(me, head, full_tiles, row_tiles)
        prior_copy(prior.at[head], partner, head, 0, partner).wait_recv()
        carry(partner, head, 0, row_tiles)

    first_offset, lead = place(me)
    for head in range(heads):
        keys_turned = transposed(key_rows[head])
        chunks = padded_keys // LANES
        for chunk in range(chunks):
            piece = keys_turned[:, chunk * LANES : (chunk + 1) * LANES]
            turned[head, chunk, pl.ds(0, LANES), :] = piece
            turned[head, chunk, pl.ds(LANES, LANES), :] = piece

        def state_block(block):
            row = lax.broadcasted_iota(jnp.int32, (LANES, LANES), 0)
            early = row < LANES - lead
            plain = jnp.logical_and(early, first_offset + block == 0)
            factor = jnp.where(plain, 1.0, ROOT_TWO)
            near_row = lax.rem(lead + first_offset + block, LANES)
            far_row = lax.rem(lead + first_offset + block + 1, LANES)
            pieces = []
            for chunk in range(chunks):
                here = turned[head, chunk, pl.ds(lead, LANES), :]
                near = turned[head, chunk, pl.ds(near_row, LANES), :]
                far = turned[head, chunk, pl.ds(far_row, LANES), :]
                both = jnp.where(early, near, far) * factor
                pieces.append((here * both).astype(jnp.bfloat16))
            features = jnp.concatenate(pieces, axis=1)
            return jnp.dot(features, value_rows[head], preferred_element_type=jnp.float32)

        whole_blocks = state_rows // LANES

        @pl.loop(0, whole_blocks)
        def _(block):
            state[head, pl.ds(pl.multiple_of(block * LANES, LANES), LANES), :] = state_block(block)

        rest = state_rows - whole_blocks * LANES
        if rest > 0:
            state[head, pl.ds(whole_blocks * LANES, rest), :] = state_block(whole_blocks)[:rest]

        @pl.loop(0, row_tiles)
        def _(tile):
            rows = pl.ds(pl.multiple_of(tile * TILE, TILE), TILE)
            scores = lax.dot_general(
                query_rows[head, rows, :],
                key_rows[head],
                contract_last,
                preferred_element_type=jnp.float32,
            )
            local = tile * TILE + lax.broadcasted_iota(jnp.int32, (TILE, 1), 0)
            position = jnp.where(
                local < window_rows,
                local + me * window_rows,
                local - window_rows + window * group + me * (per_shard * group),
            )
            key_index = lax.broadcasted_iota(jnp.int32, scores.shape, 1)
            allowed = position >= key_index * group
            weights = jnp.where(allowed, scores * scores, 0.0).astype(jnp.bfloat16)
            out[head, rows, :] = jnp.dot(
                weights, value_rows[head], preferred_element_type=jnp.float32
            )

    for step in range(1, chips):
        source = across(step)
        for head in range(heads):
            prior_copy(prior.at[head], source, head, 0, partner).wait_recv()
            prior_forward(step, head).start()
            carry(source, head, 0, row_tiles)
            prior_copy(prior.at[head], twin(source), head, 0, partner).wait_recv()
            carry(twin(source), head, 0, row_tiles)

    for head in range(heads):
        for tile in range(row_tiles):
            out[head, pl.ds(tile * TILE, TILE), :] += total_turned[head, tile].T

    for slot in range(chips):
        blob_own(slot).wait_send()
        for head in range(heads):
            prior_own(slot, head).wait_send()
    for step in range(1, chips):
        blob_forward(step).wait_send()
        for head in range(heads):
            prior_forward(step, head).wait_send()


def combine(sizes, queries, blob, prior, out_rows):
    n, heads, group, tok_rows, step_count, rows_valid = sizes
    lead = max(source * rows_valid % LANES for source in range(n))
    padded_rows = round_up(lead + rows_valid, LANES)
    chunks = out_rows // LANES
    state_rows = round_up(rows_valid, 8)
    padded_keys = round_up(n * tok_rows + step_count, LANES)
    slots = 2 * (n // 2) - 1
    vmem = pl.BlockSpec(memory_space=pltpu.VMEM)
    return pl.pallas_call(
        functools.partial(main_kernel, sizes),
        out_shape=(
            jax.ShapeDtypeStruct((heads, out_rows, LANES), jnp.float32),
            jax.ShapeDtypeStruct((heads, state_rows, LANES), jnp.float32),
        ),
        in_specs=[vmem] * 3,
        out_specs=(vmem, vmem),
        scratch_shapes=[
            pltpu.VMEM((n,) + blob.shape, jnp.bfloat16),
            pltpu.VMEM((n, heads, padded_rows, LANES), jnp.bfloat16),
            pltpu.VMEM((heads, out_rows, LANES), jnp.bfloat16),
            pltpu.VMEM((heads, chunks, LANES, LANES), jnp.float32),
            pltpu.VMEM((heads, chunks, 2 * LANES, LANES), jnp.float32),
            pltpu.VMEM((LANES, padded_rows), jnp.bfloat16),
            pltpu.VMEM((heads, out_rows // TILE, LANES, TILE), jnp.float32),
            pltpu.VMEM((heads, step_count * group, LANES), jnp.float32),
            pltpu.VMEM((heads, padded_keys, LANES), jnp.bfloat16),
            pltpu.VMEM((heads, padded_keys, LANES), jnp.bfloat16),
            pltpu.VMEM((heads, padded_keys // LANES, 2 * LANES, LANES), jnp.float32),
            pltpu.SemaphoreType.DMA((slots,)),
            pltpu.SemaphoreType.DMA((n,)),
            pltpu.SemaphoreType.DMA((slots, heads)),
            pltpu.SemaphoreType.DMA((n, heads)),
            pltpu.SemaphoreType.DMA((2,)),
        ],
        compiler_params=pltpu.CompilerParams(
            collective_id=0, has_side_effects=True, vmem_limit_bytes=56 * 2**20
        ),
        name="combine",
    )(queries, blob, prior)


def on_device(queries, keys_values, prior_state, counts, continuation, query_table, pair_table):
    tok_rows, heads, group, head_size = queries.shape
    n = lax.axis_size("ctx")
    shard_index = lax.axis_index("ctx")
    step_count = continuation.shape[0]
    per_shard = step_count // n
    rows_valid = prior_state.shape[1]

    vocab_rows = query_table.shape[0]
    local_ids = continuation - shard_index * vocab_rows
    inside = (local_ids >= 0) & (local_ids < vocab_rows)
    safe_ids = jnp.clip(local_ids, 0, vocab_rows - 1)
    query_pick, pair_pick = pick_rows(safe_ids, query_table.transpose(0, 2, 1, 3), pair_table)
    mask = inside[:, None, None, None]
    query_pick = jnp.where(mask, query_pick, jnp.zeros_like(query_pick))
    pair_pick = jnp.where(mask, pair_pick, jnp.zeros_like(pair_pick))

    window_planes = keys_values.transpose(2, 1, 0, 3).reshape(2 * heads, tok_rows, head_size)
    step_planes = pair_pick.transpose(2, 1, 0, 3)
    step_planes = step_planes.reshape(2 * heads, step_count, head_size)
    query_planes = query_pick.transpose(2, 0, 1, 3).reshape(
        2 * heads, step_count * group // 2, head_size
    )
    blob = jnp.concatenate([window_planes, step_planes, query_planes], axis=1)
    query_planes = queries.transpose(1, 0, 2, 3).reshape(heads, tok_rows * group, head_size)
    prior = prior_state
    if rows_valid % 16 != 0:
        leads = [source * rows_valid % LANES for source in range(n)]
        prior = lax.dynamic_update_slice(
            jnp.zeros((heads, round_up(max(leads) + rows_valid, LANES), LANES), prior.dtype),
            prior_state,
            (0, shard_index * rows_valid % LANES, 0),
        )
    out_rows = round_up((tok_rows + per_shard) * group, TILE)
    sizes = (n, heads, group, tok_rows, step_count, rows_valid)
    total, added = combine(sizes, query_planes, blob, prior, out_rows)

    decode_state = prior_state.astype(jnp.float32) + added[:, :rows_valid]

    def finish(rows, first_position):
        count = rows.shape[1] // group
        positions = first_position + jnp.arange(count, dtype=jnp.int32) + 1
        scale = 1.0 / (head_size * jnp.sqrt(positions.astype(jnp.float32)))
        rows = rows.reshape(heads, count, group, head_size) * scale[None, :, None, None]
        return rows.astype(jnp.bfloat16).transpose(1, 0, 2, 3)

    window_rows = tok_rows * group
    readout = finish(total[:, :window_rows], counts[0] + shard_index * tok_rows)
    decode_out = finish(
        total[:, window_rows : window_rows + per_shard * group],
        counts[0] + n * tok_rows + shard_index * per_shard,
    )
    return (readout, decode_out, decode_state)


def solution(mesh):
    in_specs = (
        P(("groups", "ctx"), "head", None, None),
        P(("groups", "ctx"), "head", None, None),
        P(("groups", "head"), "ctx", None),
        P("groups"),
        P("groups"),
        P("ctx", "head", None, None),
        P("ctx", "head", None, None),
    )
    out_specs = (
        P(("groups", "ctx"), "head", None, None),
        P(("groups", "ctx"), "head", None, None),
        P(("groups", "head"), "ctx", None),
    )
    return jax.shard_map(
        on_device, mesh=mesh, in_specs=in_specs, out_specs=out_specs, check_vma=False
    )
```

```python
import functools

import jax
import jax.numpy as jnp
from jax import lax
from jax.experimental import pallas as pl
from jax.experimental.pallas import tpu as pltpu
from jax.sharding import PartitionSpec as P

ROOT_TWO = 2.0**0.5
MESH = pl.DeviceIdType.MESH
TILE = 256
LANES = 128


def round_up(number, multiple):
    return (number + multiple - 1) // multiple * multiple


def pick_kernel(ids_ref, query_table, pair_table, query_out, pair_out, query_sem, pair_sem):
    vocab_rows = query_table.shape[0]
    first_row = lax.axis_index("ctx") * vocab_rows
    query_out[...] = jnp.zeros_like(query_out)
    pair_out[...] = jnp.zeros_like(pair_out)

    def each(step, act):
        row = ids_ref[step] - first_row

        @pl.when(jnp.logical_and(row >= 0, row < vocab_rows))
        def _():
            act(pltpu.make_async_copy(query_table.at[row], query_out.at[step], query_sem.at[step]))
            act(pltpu.make_async_copy(pair_table.at[row], pair_out.at[step], pair_sem.at[step]))

    for step in range(query_out.shape[0]):
        each(step, lambda copy: copy.start())
    for step in range(query_out.shape[0]):
        each(step, lambda copy: copy.wait())


def pick_rows(ids, query_table, pair_table):
    steps = ids.shape[0]
    return pl.pallas_call(
        pick_kernel,
        out_shape=(
            jax.ShapeDtypeStruct((steps,) + query_table.shape[1:], query_table.dtype),
            jax.ShapeDtypeStruct((steps,) + pair_table.shape[1:], pair_table.dtype),
        ),
        in_specs=[
            pl.BlockSpec(memory_space=pltpu.SMEM),
            pl.BlockSpec(memory_space=pl.ANY),
            pl.BlockSpec(memory_space=pl.ANY),
        ],
        out_specs=(
            pl.BlockSpec(memory_space=pltpu.VMEM),
            pl.BlockSpec(memory_space=pltpu.VMEM),
        ),
        scratch_shapes=[pltpu.SemaphoreType.DMA((steps,)), pltpu.SemaphoreType.DMA((steps,))],
        name="pick_rows",
    )(ids, query_table, pair_table)


def main_kernel(
    sizes,
    counts,
    queries,
    blob,
    prior,
    window_out,
    step_out,
    state_out,
    out,
    state,
    land_blob,
    land_prior,
    query_rows,
    query_plain,
    query_scaled,
    prior_turned,
    total_turned,
    step_rows,
    key_rows,
    value_rows,
    turned,
    blob_send,
    blob_recv,
    prior_send,
    prior_recv,
    local_sem,
):
    n, heads, group, tok_rows, step_count, rows_valid = sizes
    chips = n // 2
    per_shard = step_count // n
    window_rows = tok_rows * group
    window = n * tok_rows
    prior_rows = prior.shape[1]
    shifted = prior_rows == rows_valid
    state_rows = state.shape[1]
    blocks = land_prior.shape[2] // LANES
    row_tiles = out.shape[1] // TILE
    padded_keys = key_rows.shape[1]
    me = lax.axis_index("ctx")
    core = lax.rem(me, 2)
    partner = me + 1 - 2 * core

    def across(step):
        return lax.rem(me + 2 * step, n)

    def twin(index):
        return index + 1 - 2 * lax.rem(index, 2)

    barrier = pltpu.get_barrier_semaphore()
    pl.semaphore_signal(barrier, inc=1, device_id={"ctx": partner}, device_id_type=MESH)
    for step in range(1, chips):
        pl.semaphore_signal(barrier, inc=1, device_id={"ctx": across(step)}, device_id_type=MESH)
    pl.semaphore_wait(barrier, chips)

    def blob_copy(src, source, slot, target):
        return pltpu.make_async_remote_copy(
            src_ref=src,
            dst_ref=land_blob.at[source],
            send_sem=blob_send.at[slot],
            recv_sem=blob_recv.at[source],
            device_id={"ctx": target},
            device_id_type=MESH,
        )

    def landing(source):
        first = pl.multiple_of(lax.rem(source * rows_valid, LANES), 16) if shifted else 0
        return pl.ds(first, prior_rows)

    def prior_copy(src, source, head, slot, target):
        return pltpu.make_async_remote_copy(
            src_ref=src,
            dst_ref=land_prior.at[source, head, landing(source)],
            send_sem=prior_send.at[slot, head],
            recv_sem=prior_recv.at[source, head],
            device_id={"ctx": target},
            device_id_type=MESH,
        )

    def blob_own(slot):
        return blob_copy(blob, me, slot, partner if slot == 0 else across(slot))

    def blob_forward(step):
        source = across(step)
        return blob_copy(land_blob.at[source], source, chips - 1 + step, partner)

    def prior_own(slot, head):
        target = partner if slot == 0 else across(slot)
        return prior_copy(prior.at[head], me, head, slot, target)

    def prior_forward(step, head):
        source = across(step)
        return prior_copy(
            land_prior.at[source, head, landing(source)],
            source,
            head,
            chips - 1 + step,
            partner,
        )

    for slot in list(range(1, chips)) + [0]:
        blob_own(slot).start()
    for head in range(heads):
        for slot in list(range(1, chips)) + [0]:
            prior_own(slot, head).start()
    own_blob = pltpu.make_async_copy(blob, land_blob.at[me], local_sem.at[0])
    own_prior = pltpu.make_async_copy(
        prior, land_prior.at[me, :, landing(me)], local_sem.at[1]
    )
    own_blob.start()
    own_prior.start()

    if shifted:
        for source in range(n):
            lead_rows = source * rows_valid % LANES
            for first, last in (
                (0, lead_rows),
                (lead_rows + prior_rows, blocks * LANES),
            ):
                if last > first:
                    for head in range(heads):
                        land_prior[source, head, pl.ds(first, last - first), :] = jnp.zeros(
                            (last - first, LANES), jnp.bfloat16
                        )
    total_turned[...] = jnp.zeros_like(total_turned)
    for head in range(heads):
        query_rows[head, pl.ds(0, window_rows), :] = queries[head]
        query_rows[head, pl.ds(window_rows, out.shape[1] - window_rows), :] = jnp.zeros(
            (out.shape[1] - window_rows, LANES), jnp.bfloat16
        )
        spare = padded_keys - window - step_count
        if spare > 0:
            key_rows[head, pl.ds(window + step_count, spare), :] = jnp.zeros(
                (spare, LANES), jnp.bfloat16
            )
            value_rows[head, pl.ds(window + step_count, spare), :] = jnp.zeros(
                (spare, LANES), jnp.bfloat16
            )

    def place(source):
        first = source * rows_valid
        return lax.div(first, LANES), lax.rem(first, LANES)

    identity = (
        lax.broadcasted_iota(jnp.int32, (LANES, LANES), 0)
        == lax.broadcasted_iota(jnp.int32, (LANES, LANES), 1)
    ).astype(jnp.bfloat16)
    contract_last = (((1,), (1,)), ((), ()))

    def transposed(rows):
        return lax.dot_general(identity, rows, contract_last, preferred_element_type=jnp.float32)

    chunks_per_tile = TILE // LANES

    def turn_queries(head, first_tile, last_tile):
        for chunk in range(first_tile * chunks_per_tile, last_tile * chunks_per_tile):
            piece = transposed(query_rows[head, pl.ds(chunk * LANES, LANES), :])
            scaled = piece * ROOT_TWO
            query_plain[head, chunk] = piece
            query_scaled[head, chunk, pl.ds(0, LANES), :] = scaled
            query_scaled[head, chunk, pl.ds(LANES, LANES), :] = scaled

    def carry_tile(source, head, tile):
        first_offset, _ = place(source)
        columns = []
        for side in range(chunks_per_tile):
            chunk = tile * chunks_per_tile + side
            here = query_plain[head, chunk]
            pieces = []
            for block in range(blocks):
                row = lax.rem(first_offset + block, LANES)
                other = query_scaled[head, chunk, pl.ds(row, LANES), :]
                if block == 0:
                    other = jnp.where(first_offset == 0, here, other)
                pieces.append((here * other).astype(jnp.bfloat16))
            columns.append(jnp.concatenate(pieces, axis=0))
        features = jnp.concatenate(columns, axis=1)
        total_turned[head, tile] += jnp.dot(
            prior_turned[...], features, preferred_element_type=jnp.float32
        )

    def carry(source, head, first_tile, last_tile):
        prior_turned[...] = transposed(land_prior[source, head]).astype(jnp.bfloat16)

        @pl.loop(first_tile, last_tile)
        def _(tile):
            carry_tile(source, head, tile)

    full_tiles = window_rows // TILE
    own_prior.wait()
    for head in range(heads):
        turn_queries(head, 0, full_tiles)
        carry(me, head, 0, full_tiles)

    own_blob.wait()
    blob_copy(blob, partner, 0, partner).wait_recv()
    for step in range(1, chips):
        blob_copy(blob, across(step), 0, partner).wait_recv()
        blob_forward(step).start()
    for step in range(1, chips):
        blob_copy(blob, twin(across(step)), 0, partner).wait_recv()

    for head in range(heads):
        for source in range(n):
            key_rows[head, pl.ds(source * tok_rows, tok_rows), :] = land_blob[
                source, head, pl.ds(0, tok_rows), :
            ]
            value_rows[head, pl.ds(source * tok_rows, tok_rows), :] = land_blob[
                source, heads + head, pl.ds(0, tok_rows), :
            ]

        def picked(plane, first, count):
            total = land_blob[0, plane, pl.ds(first, count), :].astype(jnp.float32)
            for source in range(1, n):
                total += land_blob[source, plane, pl.ds(first, count), :].astype(jnp.float32)
            return total

        key_rows[head, pl.ds(window, step_count), :] = picked(head, tok_rows, step_count).astype(
            jnp.bfloat16
        )
        value_rows[head, pl.ds(window, step_count), :] = picked(
            heads + head, tok_rows, step_count
        ).astype(jnp.bfloat16)
        half = step_count * group // 2
        for side in range(2):
            step_rows[head, pl.ds(side * half, half), :] = picked(
                2 * head + side, tok_rows + step_count, half
            )
        own_steps = per_shard * group
        own_rows = step_rows[head, pl.ds(me * own_steps, own_steps), :]
        query_rows[head, pl.ds(window_rows, own_steps), :] = own_rows.astype(jnp.bfloat16)
        turn_queries(head, full_tiles, row_tiles)

    for head in range(heads):
        carry(me, head, full_tiles, row_tiles)
        prior_copy(prior.at[head], partner, head, 0, partner).wait_recv()
        carry(partner, head, 0, row_tiles)

    def state_copy(head):
        return pltpu.make_async_copy(state.at[head], state_out.at[head], local_sem.at[2 + head])

    def positions(tile):
        local = tile * TILE + lax.broadcasted_iota(jnp.int32, (TILE, 1), 0)
        return jnp.where(
            local < window_rows,
            local + me * window_rows,
            local - window_rows + window * group + me * (per_shard * group),
        )

    first_offset, lead = place(me)
    for head in range(heads):
        keys_turned = transposed(key_rows[head])
        chunks = padded_keys // LANES
        for chunk in range(chunks):
            piece = keys_turned[:, chunk * LANES : (chunk + 1) * LANES]
            turned[head, chunk, pl.ds(0, LANES), :] = piece
            turned[head, chunk, pl.ds(LANES, LANES), :] = piece

        def state_block(block):
            row = lax.broadcasted_iota(jnp.int32, (LANES, LANES), 0)
            early = row < LANES - lead
            plain = jnp.logical_and(early, first_offset + block == 0)
            factor = jnp.where(plain, 1.0, ROOT_TWO)
            near_row = lax.rem(lead + first_offset + block, LANES)
            far_row = lax.rem(lead + first_offset + block + 1, LANES)
            pieces = []
            for chunk in range(chunks):
                here = turned[head, chunk, pl.ds(lead, LANES), :]
                near = turned[head, chunk, pl.ds(near_row, LANES), :]
                far = turned[head, chunk, pl.ds(far_row, LANES), :]
                both = jnp.where(early, near, far) * factor
                pieces.append((here * both).astype(jnp.bfloat16))
            features = jnp.concatenate(pieces, axis=1)
            return jnp.dot(features, value_rows[head], preferred_element_type=jnp.float32)

        def before(rows):
            return prior[head, rows, :].astype(jnp.float32) if shifted else 0.0

        whole_blocks = state_rows // LANES

        @pl.loop(0, whole_blocks)
        def _(block):
            rows = pl.ds(pl.multiple_of(block * LANES, LANES), LANES)
            state[head, rows, :] = before(rows) + state_block(block)

        rest = state_rows - whole_blocks * LANES
        if rest > 0:
            rows = pl.ds(whole_blocks * LANES, rest)
            state[head, rows, :] = before(rows) + state_block(whole_blocks)[:rest]
        state_copy(head).start()

        @pl.loop(0, row_tiles)
        def _(tile):
            rows = pl.ds(pl.multiple_of(tile * TILE, TILE), TILE)
            scores = lax.dot_general(
                query_rows[head, rows, :],
                key_rows[head],
                contract_last,
                preferred_element_type=jnp.float32,
            )
            position = positions(tile)
            key_index = lax.broadcasted_iota(jnp.int32, scores.shape, 1)
            allowed = position >= key_index * group
            weights = jnp.where(allowed, scores * scores, 0.0).astype(jnp.bfloat16)
            out[head, rows, :] = jnp.dot(
                weights, value_rows[head], preferred_element_type=jnp.float32
            )

    for step in range(1, chips):
        source = across(step)
        for head in range(heads):
            prior_copy(prior.at[head], source, head, 0, partner).wait_recv()
            prior_forward(step, head).start()
            carry(source, head, 0, row_tiles)
            prior_copy(prior.at[head], twin(source), head, 0, partner).wait_recv()
            carry(twin(source), head, 0, row_tiles)

    for head in range(heads):
        for tile in range(row_tiles):
            first = tile * TILE
            token = jnp.floor((positions(tile).astype(jnp.float32) + 0.5) / group)
            place_in_prompt = token + (counts[0] + 1).astype(jnp.float32)
            scale = 1.0 / (LANES * jnp.sqrt(place_in_prompt))
            total = out[head, pl.ds(first, TILE), :] + total_turned[head, tile].T
            total = (total * scale).astype(jnp.bfloat16)
            split = min(max(window_rows - first, 0), TILE)
            if split > 0:
                window_out[head, pl.ds(first, split), :] = total[:split]
            if split < TILE:
                step_out[head, pl.ds(first + split - window_rows, TILE - split), :] = total[split:]
        state_copy(head).wait()

    for slot in range(chips):
        blob_own(slot).wait_send()
        for head in range(heads):
            prior_own(slot, head).wait_send()
    for step in range(1, chips):
        blob_forward(step).wait_send()
        for head in range(heads):
            prior_forward(step, head).wait_send()


def combine(sizes, counts, queries, blob, prior, out_rows):
    n, heads, group, tok_rows, step_count, rows_valid = sizes
    window_rows = tok_rows * group
    lead = max(source * rows_valid % LANES for source in range(n))
    padded_rows = round_up(lead + rows_valid, LANES)
    chunks = out_rows // LANES
    state_rows = round_up(rows_valid, 8)
    padded_keys = round_up(n * tok_rows + step_count, LANES)
    slots = 2 * (n // 2) - 1
    vmem = pl.BlockSpec(memory_space=pltpu.VMEM)
    return pl.pallas_call(
        functools.partial(main_kernel, sizes),
        out_shape=(
            jax.ShapeDtypeStruct((heads, window_rows, LANES), jnp.bfloat16),
            jax.ShapeDtypeStruct((heads, out_rows - window_rows, LANES), jnp.bfloat16),
            jax.ShapeDtypeStruct((heads, state_rows, LANES), jnp.float32),
        ),
        in_specs=[pl.BlockSpec(memory_space=pltpu.SMEM)] + [vmem] * 3,
        out_specs=(vmem, vmem, pl.BlockSpec(memory_space=pl.ANY)),
        scratch_shapes=[
            pltpu.VMEM((heads, out_rows, LANES), jnp.float32),
            pltpu.VMEM((heads, state_rows, LANES), jnp.float32),
            pltpu.VMEM((n,) + blob.shape, jnp.bfloat16),
            pltpu.VMEM((n, heads, padded_rows, LANES), jnp.bfloat16),
            pltpu.VMEM((heads, out_rows, LANES), jnp.bfloat16),
            pltpu.VMEM((heads, chunks, LANES, LANES), jnp.float32),
            pltpu.VMEM((heads, chunks, 2 * LANES, LANES), jnp.float32),
            pltpu.VMEM((LANES, padded_rows), jnp.bfloat16),
            pltpu.VMEM((heads, out_rows // TILE, LANES, TILE), jnp.float32),
            pltpu.VMEM((heads, step_count * group, LANES), jnp.float32),
            pltpu.VMEM((heads, padded_keys, LANES), jnp.bfloat16),
            pltpu.VMEM((heads, padded_keys, LANES), jnp.bfloat16),
            pltpu.VMEM((heads, padded_keys // LANES, 2 * LANES, LANES), jnp.float32),
            pltpu.SemaphoreType.DMA((slots,)),
            pltpu.SemaphoreType.DMA((n,)),
            pltpu.SemaphoreType.DMA((slots, heads)),
            pltpu.SemaphoreType.DMA((n, heads)),
            pltpu.SemaphoreType.DMA((2 + heads,)),
        ],
        compiler_params=pltpu.CompilerParams(
            collective_id=0, has_side_effects=True, vmem_limit_bytes=56 * 2**20
        ),
        name="combine",
    )(counts, queries, blob, prior)


def on_device(queries, keys_values, prior_state, counts, continuation, query_table, pair_table):
    tok_rows, heads, group, head_size = queries.shape
    n = lax.axis_size("ctx")
    shard_index = lax.axis_index("ctx")
    step_count = continuation.shape[0]
    per_shard = step_count // n
    rows_valid = prior_state.shape[1]

    query_pick, pair_pick = pick_rows(
        continuation, query_table.transpose(0, 2, 1, 3), pair_table
    )

    window_planes = keys_values.transpose(2, 1, 0, 3).reshape(2 * heads, tok_rows, head_size)
    step_planes = pair_pick.transpose(2, 1, 0, 3)
    step_planes = step_planes.reshape(2 * heads, step_count, head_size)
    query_planes = query_pick.transpose(2, 0, 1, 3).reshape(
        2 * heads, step_count * group // 2, head_size
    )
    blob = jnp.concatenate([window_planes, step_planes, query_planes], axis=1)
    query_planes = queries.transpose(1, 0, 2, 3).reshape(heads, tok_rows * group, head_size)
    prior = prior_state
    if rows_valid % 16 != 0:
        leads = [source * rows_valid % LANES for source in range(n)]
        prior = lax.dynamic_update_slice(
            jnp.zeros((heads, round_up(max(leads) + rows_valid, LANES), LANES), prior.dtype),
            prior_state,
            (0, shard_index * rows_valid % LANES, 0),
        )
    out_rows = round_up((tok_rows + per_shard) * group, TILE)
    sizes = (n, heads, group, tok_rows, step_count, rows_valid)
    window_out, step_out, state = combine(sizes, counts, query_planes, blob, prior, out_rows)

    decode_state = state
    if rows_valid % 16 != 0:
        decode_state = prior_state.astype(jnp.float32) + state[:, :rows_valid]
    readout = window_out.reshape(heads, tok_rows, group, head_size).transpose(1, 0, 2, 3)
    decode_out = step_out[:, : per_shard * group]
    decode_out = decode_out.reshape(heads, per_shard, group, head_size).transpose(1, 0, 2, 3)
    return (readout, decode_out, decode_state)


def solution(mesh):
    in_specs = (
        P(("groups", "ctx"), "head", None, None),
        P(("groups", "ctx"), "head", None, None),
        P(("groups", "head"), "ctx", None),
        P("groups"),
        P("groups"),
        P("ctx", "head", None, None),
        P("ctx", "head", None, None),
    )
    out_specs = (
        P(("groups", "ctx"), "head", None, None),
        P(("groups", "ctx"), "head", None, None),
        P(("groups", "head"), "ctx", None),
    )
    return jax.shard_map(
        on_device, mesh=mesh, in_specs=in_specs, out_specs=out_specs, check_vma=False
    )
```

```python
import functools

import jax
import jax.numpy as jnp
from jax import lax
from jax.experimental import pallas as pl
from jax.experimental.pallas import tpu as pltpu
from jax.sharding import PartitionSpec as P

ROOT_TWO = 2.0**0.5
MESH = pl.DeviceIdType.MESH
TILE = 256
LANES = 128


def round_up(number, multiple):
    return (number + multiple - 1) // multiple * multiple


def pick_kernel(ids_ref, query_table, pair_table, query_out, pair_out, query_sem, pair_sem):
    vocab_rows = query_table.shape[0]
    first_row = lax.axis_index("ctx") * vocab_rows
    query_out[...] = jnp.zeros_like(query_out)
    pair_out[...] = jnp.zeros_like(pair_out)

    def each(step, act):
        row = ids_ref[step] - first_row

        @pl.when(jnp.logical_and(row >= 0, row < vocab_rows))
        def _():
            act(pltpu.make_async_copy(query_table.at[row], query_out.at[step], query_sem.at[step]))
            act(pltpu.make_async_copy(pair_table.at[row], pair_out.at[step], pair_sem.at[step]))

    for step in range(query_out.shape[0]):
        each(step, lambda copy: copy.start())
    for step in range(query_out.shape[0]):
        each(step, lambda copy: copy.wait())


def pick_rows(ids, query_table, pair_table):
    steps = ids.shape[0]
    return pl.pallas_call(
        pick_kernel,
        out_shape=(
            jax.ShapeDtypeStruct((steps,) + query_table.shape[1:], query_table.dtype),
            jax.ShapeDtypeStruct((steps,) + pair_table.shape[1:], pair_table.dtype),
        ),
        in_specs=[
            pl.BlockSpec(memory_space=pltpu.SMEM),
            pl.BlockSpec(memory_space=pl.ANY),
            pl.BlockSpec(memory_space=pl.ANY),
        ],
        out_specs=(
            pl.BlockSpec(memory_space=pltpu.VMEM),
            pl.BlockSpec(memory_space=pltpu.VMEM),
        ),
        scratch_shapes=[pltpu.SemaphoreType.DMA((steps,)), pltpu.SemaphoreType.DMA((steps,))],
        name="pick_rows",
    )(ids, query_table, pair_table)


def main_kernel(
    sizes,
    counts,
    queries,
    blob,
    prior,
    window_out,
    step_out,
    state_out,
    out,
    state,
    land_blob,
    land_prior,
    query_rows,
    query_plain,
    query_scaled,
    prior_turned,
    total_turned,
    step_rows,
    key_rows,
    value_rows,
    turned,
    blob_send,
    blob_recv,
    prior_send,
    prior_recv,
    local_sem,
):
    n, heads, group, tok_rows, step_count, rows_valid = sizes
    chips = n // 2
    per_shard = step_count // n
    window_rows = tok_rows * group
    window = n * tok_rows
    prior_rows = prior.shape[1]
    shifted = prior_rows == rows_valid
    state_rows = state.shape[1]
    blocks = land_prior.shape[2] // LANES
    row_tiles = out.shape[1] // TILE
    padded_keys = key_rows.shape[1]
    me = lax.axis_index("ctx")
    core = lax.rem(me, 2)
    partner = me + 1 - 2 * core

    def across(step):
        return lax.rem(me + 2 * step, n)

    def twin(index):
        return index + 1 - 2 * lax.rem(index, 2)

    barrier = pltpu.get_barrier_semaphore()
    pl.semaphore_signal(barrier, inc=1, device_id={"ctx": partner}, device_id_type=MESH)
    for step in range(1, chips):
        pl.semaphore_signal(barrier, inc=1, device_id={"ctx": across(step)}, device_id_type=MESH)
    pl.semaphore_wait(barrier, chips)

    def blob_copy(src, source, slot, target):
        return pltpu.make_async_remote_copy(
            src_ref=src,
            dst_ref=land_blob.at[source],
            send_sem=blob_send.at[slot],
            recv_sem=blob_recv.at[source],
            device_id={"ctx": target},
            device_id_type=MESH,
        )

    def landing(source):
        first = pl.multiple_of(lax.rem(source * rows_valid, LANES), 16) if shifted else 0
        return pl.ds(first, prior_rows)

    def prior_copy(src, source, head, slot, target):
        return pltpu.make_async_remote_copy(
            src_ref=src,
            dst_ref=land_prior.at[source, head, landing(source)],
            send_sem=prior_send.at[slot, head],
            recv_sem=prior_recv.at[source, head],
            device_id={"ctx": target},
            device_id_type=MESH,
        )

    def blob_own(slot):
        return blob_copy(blob, me, slot, partner if slot == 0 else across(slot))

    def blob_forward(step):
        source = across(step)
        return blob_copy(land_blob.at[source], source, chips - 1 + step, partner)

    def prior_own(slot, head):
        target = partner if slot == 0 else across(slot)
        return prior_copy(prior.at[head], me, head, slot, target)

    def prior_forward(step, head):
        source = across(step)
        return prior_copy(
            land_prior.at[source, head, landing(source)],
            source,
            head,
            chips - 1 + step,
            partner,
        )

    for slot in list(range(1, chips)) + [0]:
        blob_own(slot).start()
    for head in range(heads):
        for slot in list(range(1, chips)) + [0]:
            prior_own(slot, head).start()
    own_blob = pltpu.make_async_copy(blob, land_blob.at[me], local_sem.at[0])
    own_prior = pltpu.make_async_copy(
        prior, land_prior.at[me, :, landing(me)], local_sem.at[1]
    )
    own_blob.start()
    own_prior.start()

    if shifted:
        for source in range(n):
            lead_rows = source * rows_valid % LANES
            for first, last in (
                (0, lead_rows),
                (lead_rows + prior_rows, blocks * LANES),
            ):
                if last > first:
                    for head in range(heads):
                        land_prior[source, head, pl.ds(first, last - first), :] = jnp.zeros(
                            (last - first, LANES), jnp.bfloat16
                        )
    total_turned[...] = jnp.zeros_like(total_turned)
    for head in range(heads):
        query_rows[head, pl.ds(0, window_rows), :] = queries[head]
        query_rows[head, pl.ds(window_rows, out.shape[1] - window_rows), :] = jnp.zeros(
            (out.shape[1] - window_rows, LANES), jnp.bfloat16
        )
        spare = padded_keys - window - step_count
        if spare > 0:
            key_rows[head, pl.ds(window + step_count, spare), :] = jnp.zeros(
                (spare, LANES), jnp.bfloat16
            )
            value_rows[head, pl.ds(window + step_count, spare), :] = jnp.zeros(
                (spare, LANES), jnp.bfloat16
            )

    def place(source):
        first = source * rows_valid
        return lax.div(first, LANES), lax.rem(first, LANES)

    identity = (
        lax.broadcasted_iota(jnp.int32, (LANES, LANES), 0)
        == lax.broadcasted_iota(jnp.int32, (LANES, LANES), 1)
    ).astype(jnp.bfloat16)
    contract_last = (((1,), (1,)), ((), ()))

    def transposed(rows):
        return lax.dot_general(identity, rows, contract_last, preferred_element_type=jnp.float32)

    chunks_per_tile = TILE // LANES

    def turn_queries(head, first_tile, last_tile):
        for chunk in range(first_tile * chunks_per_tile, last_tile * chunks_per_tile):
            piece = transposed(query_rows[head, pl.ds(chunk * LANES, LANES), :])
            scaled = piece * ROOT_TWO
            query_plain[head, chunk] = piece
            query_scaled[head, chunk, pl.ds(0, LANES), :] = scaled
            query_scaled[head, chunk, pl.ds(LANES, LANES), :] = scaled

    def carry_tile(source, head, tile):
        first_offset, _ = place(source)
        columns = []
        for side in range(chunks_per_tile):
            chunk = tile * chunks_per_tile + side
            here = query_plain[head, chunk]
            pieces = []
            for block in range(blocks):
                row = lax.rem(first_offset + block, LANES)
                other = query_scaled[head, chunk, pl.ds(row, LANES), :]
                if block == 0:
                    other = jnp.where(first_offset == 0, here, other)
                pieces.append((here * other).astype(jnp.bfloat16))
            columns.append(jnp.concatenate(pieces, axis=0))
        features = jnp.concatenate(columns, axis=1)
        total_turned[head, tile] += jnp.dot(
            prior_turned[...], features, preferred_element_type=jnp.float32
        )

    def carry(source, head, first_tile, last_tile):
        prior_turned[...] = transposed(land_prior[source, head]).astype(jnp.bfloat16)

        @pl.loop(first_tile, last_tile)
        def _(tile):
            carry_tile(source, head, tile)

    full_tiles = window_rows // TILE
    own_prior.wait()
    for head in range(heads):
        turn_queries(head, 0, full_tiles)
        carry(me, head, 0, full_tiles)

    def carry_partner(head):
        prior_copy(prior.at[head], partner, head, 0, partner).wait_recv()
        carry(partner, head, 0, full_tiles)

    carry_partner(0)
    own_blob.wait()
    blob_copy(blob, partner, 0, partner).wait_recv()
    for step in range(1, chips):
        blob_copy(blob, across(step), 0, partner).wait_recv()
        blob_forward(step).start()
    for head in range(1, heads):
        carry_partner(head)
    for step in range(1, chips):
        blob_copy(blob, twin(across(step)), 0, partner).wait_recv()

    for head in range(heads):
        for source in range(n):
            key_rows[head, pl.ds(source * tok_rows, tok_rows), :] = land_blob[
                source, head, pl.ds(0, tok_rows), :
            ]
            value_rows[head, pl.ds(source * tok_rows, tok_rows), :] = land_blob[
                source, heads + head, pl.ds(0, tok_rows), :
            ]

        def picked(plane, first, count):
            total = land_blob[0, plane, pl.ds(first, count), :].astype(jnp.float32)
            for source in range(1, n):
                total += land_blob[source, plane, pl.ds(first, count), :].astype(jnp.float32)
            return total

        key_rows[head, pl.ds(window, step_count), :] = picked(head, tok_rows, step_count).astype(
            jnp.bfloat16
        )
        value_rows[head, pl.ds(window, step_count), :] = picked(
            heads + head, tok_rows, step_count
        ).astype(jnp.bfloat16)
        half = step_count * group // 2
        for side in range(2):
            step_rows[head, pl.ds(side * half, half), :] = picked(
                2 * head + side, tok_rows + step_count, half
            )
        own_steps = per_shard * group
        own_rows = step_rows[head, pl.ds(me * own_steps, own_steps), :]
        query_rows[head, pl.ds(window_rows, own_steps), :] = own_rows.astype(jnp.bfloat16)
        turn_queries(head, full_tiles, row_tiles)

    for head in range(heads):
        carry(me, head, full_tiles, row_tiles)
        carry(partner, head, full_tiles, row_tiles)

    def state_copy(head):
        return pltpu.make_async_copy(state.at[head], state_out.at[head], local_sem.at[2 + head])

    def positions(tile):
        local = tile * TILE + lax.broadcasted_iota(jnp.int32, (TILE, 1), 0)
        return jnp.where(
            local < window_rows,
            local + me * window_rows,
            local - window_rows + window * group + me * (per_shard * group),
        )

    first_offset, lead = place(me)
    for head in range(heads):
        keys_turned = transposed(key_rows[head])
        chunks = padded_keys // LANES
        for chunk in range(chunks):
            piece = keys_turned[:, chunk * LANES : (chunk + 1) * LANES]
            turned[head, chunk, pl.ds(0, LANES), :] = piece
            turned[head, chunk, pl.ds(LANES, LANES), :] = piece

        def state_block(block):
            row = lax.broadcasted_iota(jnp.int32, (LANES, LANES), 0)
            early = row < LANES - lead
            plain = jnp.logical_and(early, first_offset + block == 0)
            factor = jnp.where(plain, 1.0, ROOT_TWO)
            near_row = lax.rem(lead + first_offset + block, LANES)
            far_row = lax.rem(lead + first_offset + block + 1, LANES)
            pieces = []
            for chunk in range(chunks):
                here = turned[head, chunk, pl.ds(lead, LANES), :]
                near = turned[head, chunk, pl.ds(near_row, LANES), :]
                far = turned[head, chunk, pl.ds(far_row, LANES), :]
                both = jnp.where(early, near, far) * factor
                pieces.append((here * both).astype(jnp.bfloat16))
            features = jnp.concatenate(pieces, axis=1)
            return jnp.dot(features, value_rows[head], preferred_element_type=jnp.float32)

        def before(rows):
            return prior[head, rows, :].astype(jnp.float32) if shifted else 0.0

        whole_blocks = state_rows // LANES

        @pl.loop(0, whole_blocks)
        def _(block):
            rows = pl.ds(pl.multiple_of(block * LANES, LANES), LANES)
            state[head, rows, :] = before(rows) + state_block(block)

        rest = state_rows - whole_blocks * LANES
        if rest > 0:
            rows = pl.ds(whole_blocks * LANES, rest)
            state[head, rows, :] = before(rows) + state_block(whole_blocks)[:rest]
        state_copy(head).start()

        @pl.loop(0, row_tiles)
        def _(tile):
            rows = pl.ds(pl.multiple_of(tile * TILE, TILE), TILE)
            scores = lax.dot_general(
                query_rows[head, rows, :],
                key_rows[head],
                contract_last,
                preferred_element_type=jnp.float32,
            )
            position = positions(tile)
            key_index = lax.broadcasted_iota(jnp.int32, scores.shape, 1)
            allowed = position >= key_index * group
            weights = jnp.where(allowed, scores * scores, 0.0).astype(jnp.bfloat16)
            out[head, rows, :] = jnp.dot(
                weights, value_rows[head], preferred_element_type=jnp.float32
            )

        for step in range(1, chips):
            prior_copy(prior.at[head], across(step), head, 0, partner).wait_recv()
            prior_forward(step, head).start()

    for step in range(1, chips):
        source = across(step)
        for head in range(heads):
            carry(source, head, 0, row_tiles)
            prior_copy(prior.at[head], twin(source), head, 0, partner).wait_recv()
            carry(twin(source), head, 0, row_tiles)

    for head in range(heads):
        for tile in range(row_tiles):
            first = tile * TILE
            token = jnp.floor((positions(tile).astype(jnp.float32) + 0.5) / group)
            place_in_prompt = token + (counts[0] + 1).astype(jnp.float32)
            scale = 1.0 / (LANES * jnp.sqrt(place_in_prompt))
            total = out[head, pl.ds(first, TILE), :] + total_turned[head, tile].T
            total = (total * scale).astype(jnp.bfloat16)
            split = min(max(window_rows - first, 0), TILE)
            if split > 0:
                window_out[head, pl.ds(first, split), :] = total[:split]
            if split < TILE:
                step_out[head, pl.ds(first + split - window_rows, TILE - split), :] = total[split:]
        state_copy(head).wait()

    for slot in range(chips):
        blob_own(slot).wait_send()
        for head in range(heads):
            prior_own(slot, head).wait_send()
    for step in range(1, chips):
        blob_forward(step).wait_send()
        for head in range(heads):
            prior_forward(step, head).wait_send()


def combine(sizes, counts, queries, blob, prior, out_rows):
    n, heads, group, tok_rows, step_count, rows_valid = sizes
    window_rows = tok_rows * group
    lead = max(source * rows_valid % LANES for source in range(n))
    padded_rows = round_up(lead + rows_valid, LANES)
    chunks = out_rows // LANES
    state_rows = round_up(rows_valid, 8)
    padded_keys = round_up(n * tok_rows + step_count, LANES)
    slots = 2 * (n // 2) - 1
    vmem = pl.BlockSpec(memory_space=pltpu.VMEM)
    return pl.pallas_call(
        functools.partial(main_kernel, sizes),
        out_shape=(
            jax.ShapeDtypeStruct((heads, window_rows, LANES), jnp.bfloat16),
            jax.ShapeDtypeStruct((heads, out_rows - window_rows, LANES), jnp.bfloat16),
            jax.ShapeDtypeStruct((heads, state_rows, LANES), jnp.float32),
        ),
        in_specs=[pl.BlockSpec(memory_space=pltpu.SMEM)] + [vmem] * 3,
        out_specs=(vmem, vmem, pl.BlockSpec(memory_space=pl.ANY)),
        scratch_shapes=[
            pltpu.VMEM((heads, out_rows, LANES), jnp.float32),
            pltpu.VMEM((heads, state_rows, LANES), jnp.float32),
            pltpu.VMEM((n,) + blob.shape, jnp.bfloat16),
            pltpu.VMEM((n, heads, padded_rows, LANES), jnp.bfloat16),
            pltpu.VMEM((heads, out_rows, LANES), jnp.bfloat16),
            pltpu.VMEM((heads, chunks, LANES, LANES), jnp.float32),
            pltpu.VMEM((heads, chunks, 2 * LANES, LANES), jnp.float32),
            pltpu.VMEM((LANES, padded_rows), jnp.bfloat16),
            pltpu.VMEM((heads, out_rows // TILE, LANES, TILE), jnp.float32),
            pltpu.VMEM((heads, step_count * group, LANES), jnp.float32),
            pltpu.VMEM((heads, padded_keys, LANES), jnp.bfloat16),
            pltpu.VMEM((heads, padded_keys, LANES), jnp.bfloat16),
            pltpu.VMEM((heads, padded_keys // LANES, 2 * LANES, LANES), jnp.float32),
            pltpu.SemaphoreType.DMA((slots,)),
            pltpu.SemaphoreType.DMA((n,)),
            pltpu.SemaphoreType.DMA((slots, heads)),
            pltpu.SemaphoreType.DMA((n, heads)),
            pltpu.SemaphoreType.DMA((2 + heads,)),
        ],
        compiler_params=pltpu.CompilerParams(
            collective_id=0, has_side_effects=True, vmem_limit_bytes=56 * 2**20
        ),
        name="combine",
    )(counts, queries, blob, prior)


def on_device(queries, keys_values, prior_state, counts, continuation, query_table, pair_table):
    tok_rows, heads, group, head_size = queries.shape
    n = lax.axis_size("ctx")
    shard_index = lax.axis_index("ctx")
    step_count = continuation.shape[0]
    per_shard = step_count // n
    rows_valid = prior_state.shape[1]

    query_pick, pair_pick = pick_rows(
        continuation, query_table.transpose(0, 2, 1, 3), pair_table
    )

    window_planes = keys_values.transpose(2, 1, 0, 3).reshape(2 * heads, tok_rows, head_size)
    step_planes = pair_pick.transpose(2, 1, 0, 3)
    step_planes = step_planes.reshape(2 * heads, step_count, head_size)
    query_planes = query_pick.transpose(2, 0, 1, 3).reshape(
        2 * heads, step_count * group // 2, head_size
    )
    blob = jnp.concatenate([window_planes, step_planes, query_planes], axis=1)
    query_planes = queries.transpose(1, 0, 2, 3).reshape(heads, tok_rows * group, head_size)
    prior = prior_state
    if rows_valid % 16 != 0:
        leads = [source * rows_valid % LANES for source in range(n)]
        prior = lax.dynamic_update_slice(
            jnp.zeros((heads, round_up(max(leads) + rows_valid, LANES), LANES), prior.dtype),
            prior_state,
            (0, shard_index * rows_valid % LANES, 0),
        )
    out_rows = round_up((tok_rows + per_shard) * group, TILE)
    sizes = (n, heads, group, tok_rows, step_count, rows_valid)
    window_out, step_out, state = combine(sizes, counts, query_planes, blob, prior, out_rows)

    decode_state = state
    if rows_valid % 16 != 0:
        decode_state = prior_state.astype(jnp.float32) + state[:, :rows_valid]
    readout = window_out.reshape(heads, tok_rows, group, head_size).transpose(1, 0, 2, 3)
    decode_out = step_out[:, : per_shard * group]
    decode_out = decode_out.reshape(heads, per_shard, group, head_size).transpose(1, 0, 2, 3)
    return (readout, decode_out, decode_state)


def solution(mesh):
    in_specs = (
        P(("groups", "ctx"), "head", None, None),
        P(("groups", "ctx"), "head", None, None),
        P(("groups", "head"), "ctx", None),
        P("groups"),
        P("groups"),
        P("ctx", "head", None, None),
        P("ctx", "head", None, None),
    )
    out_specs = (
        P(("groups", "ctx"), "head", None, None),
        P(("groups", "ctx"), "head", None, None),
        P(("groups", "head"), "ctx", None),
    )
    return jax.shard_map(
        on_device, mesh=mesh, in_specs=in_specs, out_specs=out_specs, check_vma=False
    )
```
